32 devices in a mesh: pts: 4 (over x, core), snap: 8 (over z, y).
Axes of the slice: x: 2, y: 2, z: 4, core: 2. Of those that a mesh axis runs over, the one named last changes fastest.
Arguments:
- snapshots: float32 [4096, 8192], P('pts', 'snap'), may hold values from -8 to 8
- modes_init: float32 [4096, 128], P('pts'), may hold values from -6 to 6
- coefs_init: float32 [128, 8192], P(None, 'snap'), may hold values from -0.09375 to 0.09375
Outputs:
- modes: float32 [4096, 128], P('pts')
- amplitudes: float32 [128, 8192], P(None, 'snap')
The draws below stay inside these ranges and needn't reach their ends.
All inputs are finite; a program needn't handle non-finite values.
Results may differ from the reference program's by a relative error of at most 0.0003.
Values sent between devices are 32-bit elements; how exact they have to be, the bound alone decides.
A program may use at most 64 MiB of HBM per device.

```python
import jax
import jax.numpy as jnp
from jax import lax

RANK = 128
S_DEV = 1024
OUTER = 2
INNER = 2
NP = 4096
NS = 8192
N_SNAP = 8


def shard_levels(key, extent, split, least, top_value):
    loudness = 1.0
    for position, shards_of in split:
        draws = jax.random.uniform(jax.random.fold_in(jax.random.fold_in(key, 6), position), (shards_of,), jnp.float32, least / len(split), top_value / len(split))
        loudness = loudness * jnp.repeat(jnp.exp(draws), extent[position] // shards_of).reshape((-1,) + (1,) * (len(extent) - 1 - position))
    return loudness


def normal_values(key, dims, scale, most, split=(), held_as=jnp.bfloat16):
    level = shard_levels(key, dims, split, -0.22, 0.18) if split else 1.0
    entries = jax.random.normal(key, dims, jnp.float32) * scale * level
    return jnp.minimum(jnp.maximum(entries, -most), most).astype(held_as)


def setup_inputs(seed: int = 0) -> dict:
    arg_keys = jax.random.split(jax.random.key(seed), 4)
    snapshots = normal_values(arg_keys[0], (NP, NS), 1.0, 8.0, ((0, 4), (1, 8)), jnp.float32)
    modes_init = normal_values(arg_keys[1], (NP, RANK), 1.0, 6.0, ((0, 4),), jnp.float32)
    coefs_init = normal_values(arg_keys[2], (RANK, NS), NP ** -0.5, 0.09375, ((1, 8),), jnp.float32)
    return {"snapshots": snapshots, "modes_init": modes_init, "coefs_init": coefs_init}


HUBER = 1.345
RIDGE = 0.01

def high_dot(left, right):
    return jnp.dot(left.astype(jnp.float32), right.astype(jnp.float32), preferred_element_type=jnp.float32, precision=lax.Precision.HIGHEST)

def column_block(snapshots, coefs, index):
    start = (index * S_DEV).astype(jnp.int32)
    block = lax.dynamic_slice_in_dim(snapshots, start, S_DEV, 1)
    coef_block = lax.dynamic_slice_in_dim(coefs, start, S_DEV, 1)
    return (block, coef_block)

def error_block(snapshots, modes, coefs, index):
    block, coef_block = column_block(snapshots, coefs, index)
    return (block - high_dot(modes, coef_block), coef_block)

def find_limit(snapshots, modes, coefs):
    blocks = jnp.arange(N_SNAP, dtype=jnp.int32)

    def squares(index):
        error, unused = error_block(snapshots, modes, coefs, index)
        return jnp.sum(error * error)
    total = jnp.sum(lax.map(squares, blocks))
    return HUBER * jnp.sqrt(total / (NP * NS) + 1e-06)

def reference(snapshots, modes_init, coefs_init):
    modes = modes_init
    coefs = coefs_init
    eye = jnp.eye(RANK, dtype=jnp.float32)
    blocks = jnp.arange(N_SNAP, dtype=jnp.int32)
    for outer in range(OUTER):
        gram = high_dot(modes.T, modes) + RIDGE * eye
        factor = jnp.linalg.cholesky(gram)
        for inner in range(INNER):
            limit = find_limit(snapshots, modes, coefs)

            def project(index):
                error, unused = error_block(snapshots, modes, coefs, index)
                return high_dot(modes.T, jnp.clip(error, -limit, limit))
            pieces = lax.map(project, blocks)
            product = jnp.transpose(pieces, (1, 0, 2)).reshape(RANK, NS)
            coefs = coefs + jax.scipy.linalg.cho_solve((factor, True), product)
        limit = find_limit(snapshots, modes, coefs)
        hess = high_dot(coefs, coefs.T) + RIDGE * eye
        hfactor = jnp.linalg.cholesky(hess)

        def accumulate(total, index):
            error, coef_block = error_block(snapshots, modes, coefs, index)
            return (total + high_dot(jnp.clip(error, -limit, limit), coef_block.T), None)
        start_total = jnp.zeros((NP, RANK), jnp.float32)
        moment, unused = lax.scan(accumulate, start_total, blocks)
        modes = modes + jax.scipy.linalg.cho_solve((hfactor, True), moment.T).T
    return (modes, coefs * jnp.sqrt(jnp.float32(NP)))
```

```python
import functools

import jax
import jax.numpy as jnp
from jax import lax
from jax.experimental import pallas as pl
from jax.experimental.pallas import tpu as pltpu
from jax.sharding import PartitionSpec as P

OUTER = 2
INNER = 2

HUBER = 1.345
RIDGE = 0.01

F32 = jnp.float32
BF16 = jnp.bfloat16
MESH = pl.DeviceIdType.MESH


def split(x):
    hi = x.astype(BF16)
    lo = (x - hi.astype(F32)).astype(BF16)
    return hi, lo


def dot(a, b):
    return jnp.dot(a, b, preferred_element_type=F32)


def quads(x):
    r, c = x.shape[0] // 2, x.shape[1] // 2
    return (x[:r, :c] + x[:r, c:]) + (x[r:, :c] + x[r:, c:])


def pts_peer(me, j, n):
    if n % 2:
        return lax.rem(me + j, n)
    x, c = me // 2, lax.rem(me, 2)
    return lax.rem(x + j // 2, n // 2) * 2 + lax.rem(c + lax.rem(j, 2), 2)


def snap_peer(me, j, n):
    return lax.rem(me + j, n)


def kernel(n_pts, n_snap, s_hbm, m_in, c_in, m_out, c_out,
           s, e, mcat, mtcat, ccat, ctcat, sq,
           gpart, gslots, gred, gfull, hpart, hslots, hred, hfull,
           tile_p, slots_p, tile_s, slots_s, proj, proj_slots, mom, mom_slots,
           load_sem, p_send, p_recv, s_send, s_recv):
    rows, width = s.shape
    rank = m_in.shape[1]
    pme = lax.axis_index("pts")
    sme = lax.axis_index("snap")
    cw = width // n_pts
    rw = rows // n_snap
    gw = rank // n_pts
    hw = rank // n_snap
    points = float(rows * n_pts)
    count = float(rows * n_pts * width * n_snap)
    step_cols = 256
    own_cols = pl.ds(pl.multiple_of(pme * cw, cw), cw)
    own_rows = pl.ds(pl.multiple_of(sme * rw, rw), rw)

    load = pltpu.make_async_copy(s_hbm, s, load_sem)
    load.start()

    barrier = pltpu.get_barrier_semaphore()
    for j in range(1, n_pts):
        pl.semaphore_signal(barrier, inc=1, device_id={"pts": pts_peer(pme, j, n_pts)}, device_id_type=MESH)
    for j in range(1, n_snap):
        pl.semaphore_signal(barrier, inc=1, device_id={"snap": snap_peer(sme, j, n_snap)}, device_id_type=MESH)
    m_out[...] = m_in[...]
    c_out[...] = c_in[...]
    pl.semaphore_wait(barrier, n_pts - 1 + n_snap - 1)

    def pcopy(site, j, src, dst):
        return pltpu.make_async_remote_copy(
            src_ref=src, dst_ref=dst, send_sem=p_send.at[site, j - 1], recv_sem=p_recv.at[site, j - 1],
            device_id={"pts": pts_peer(pme, j, n_pts)}, device_id_type=MESH)

    def scopy(site, j, src, dst):
        return pltpu.make_async_remote_copy(
            src_ref=src, dst_ref=dst, send_sem=s_send.at[site, j - 1], recv_sem=s_recv.at[site, j - 1],
            device_id={"snap": snap_peer(sme, j, n_snap)}, device_id_type=MESH)

    def start(copies):
        for copy in copies:
            copy.start()

    def finish(copies):
        for copy in copies:
            copy.wait_recv()
        for copy in copies:
            copy.wait_send()

    def prepare_modes():
        m = m_out[...]
        hi, lo = split(m)
        mcat[:, :rank] = hi
        mcat[:, rank:] = lo
        hi, lo = split(m.T)
        mtcat[:rank, :] = hi
        mtcat[rank:, :] = lo

    def prepare_coefs():
        hi, lo = split(c_out[...])
        ccat[:rank, :] = hi
        ccat[rank:, :] = lo

    def sweep(ref, lo, hi):
        lane = lax.broadcasted_iota(jnp.int32, (rank, rank), 1)
        sub = lax.broadcasted_iota(jnp.int32, (rank, rank), 0)
        lane_row = lax.broadcasted_iota(jnp.int32, (1, rank), 1)

        def body(k, carry):
            full = ref[...]
            row = ref[pl.ds(k, 1), :]
            pivot = jnp.sum(jnp.where(lane_row == k, row, 0.0), axis=1, keepdims=True)
            col = jnp.sum(jnp.where(lane == k, full, 0.0), axis=1, keepdims=True)
            inv = 1.0 / pivot
            rowd = jnp.where(lane_row == k, -inv, row * inv)
            new = full - col * (row * inv)
            new = jnp.where(lane == k, col * inv, new)
            ref[...] = jnp.where(sub == k, rowd, new)
            return carry
        lax.fori_loop(lo, hi, body, 0)

    def error_pass():
        sq[...] = jnp.zeros_like(sq)

        def body(t, carry):
            cols = pl.ds(pl.multiple_of(t * step_cols, step_cols), step_cols)
            c = ccat[:, cols]
            hi, lo = mcat[:, :rank], mcat[:, rank:]
            fit = dot(jnp.concatenate([hi, hi], 1), c) + dot(jnp.concatenate([lo, lo], 1), c)
            err = s[:, cols] - fit
            e[:, cols] = err
            sq[...] += jnp.sum((err * err).reshape(rows // 8, 8, step_cols), axis=0)
            return carry
        lax.fori_loop(0, width // step_cols, body, 0)
        acc = sq[:, :128]
        for k in range(1, step_cols // 128):
            acc = acc + sq[:, k * 128:(k + 1) * 128]
        return acc

    def find_limit(use, acc, fill_p, fill_s):
        tile_p[use] = acc
        copies = [pcopy(use, j, tile_p.at[use], slots_p.at[use, j - 1]) for j in range(1, n_pts)]
        start(copies)
        fill_p()
        finish(copies)
        acc = tile_p[use]
        for j in range(1, n_pts):
            acc = acc + slots_p[use, j - 1]
        tile_s[use] = acc
        copies = [scopy(use, j, tile_s.at[use], slots_s.at[use, j - 1]) for j in range(1, n_snap)]
        start(copies)
        fill_s()
        finish(copies)
        acc = tile_s[use]
        for j in range(1, n_snap):
            acc = acc + slots_s[use, j - 1]
        total = jnp.sum(jnp.sum(acc, axis=0, keepdims=True), axis=1, keepdims=True)
        return HUBER * jnp.sqrt(total / count + 1e-06)

    def nothing():
        return None

    eye = (lax.broadcasted_iota(jnp.int32, (rank, rank), 0)
           == lax.broadcasted_iota(jnp.int32, (rank, rank), 1)).astype(F32) * RIDGE

    prepare_modes()
    prepare_coefs()
    load.wait()

    def outer(o, carry):
        gpart[...] = quads(dot(mtcat[...], mcat[...]))
        grs = [pcopy(3, j, gpart.at[pl.ds(pts_peer(pme, j, n_pts) * gw, gw)], gslots.at[j - 1]) for j in range(1, n_pts)]
        start(grs)
        gag = [pcopy(4, j, gred, gfull.at[pl.ds(pme * gw, gw)]) for j in range(1, n_pts)]

        for inner in range(INNER):
            acc = error_pass()

            def gram_share():
                finish(grs)
                own = gpart[pl.ds(pme * gw, gw), :]
                for j in range(1, n_pts):
                    own = own + gslots[j - 1]
                gred[...] = own
                gfull[pl.ds(pme * gw, gw), :] = own
                start(gag)

            def gram_sweep():
                finish(gag)
                gfull[...] = gfull[...] + eye
                sweep(gfull, 0, rank // 2)
            first = inner == 0
            limit = find_limit(inner, acc, gram_share if first else nothing, gram_sweep if first else nothing)

            def project(t, carry):
                j = n_pts - 1 - t
                q = pts_peer(pme, j, n_pts)
                cols = pl.ds(pl.multiple_of(q * cw, cw), cw)
                hi, lo = split(jnp.clip(e[:, cols], -limit, limit))
                proj[j] = quads(dot(mtcat[...], jnp.concatenate([hi, lo], 1)))

                @pl.when(j > 0)
                def _():
                    pcopy(5 + inner, j, proj.at[j], proj_slots.at[inner, j - 1]).start()
                return carry
            lax.fori_loop(0, n_pts, project, 0)
            if first:
                sweep(gfull, rank // 2, rank)
            finish([pcopy(5 + inner, j, proj.at[j], proj_slots.at[inner, j - 1]) for j in range(1, n_pts)])
            share = proj[0]
            for j in range(1, n_pts):
                share = share + proj_slots[inner, j - 1]
            step = jnp.dot(gfull[...], share, preferred_element_type=F32, precision=lax.Precision.HIGHEST)
            c_out[:, own_cols] = c_out[:, own_cols] - step
            copies = [pcopy(7 + inner, j, c_out.at[:, own_cols], c_out.at[:, own_cols]) for j in range(n_pts - 1, 0, -1)]
            start(copies)
            finish(copies)
            prepare_coefs()

        hi, lo = split(c_out[...].T)
        ctcat[:, :rank] = hi
        ctcat[:, rank:] = lo
        hpart[...] = quads(dot(ccat[...], ctcat[...]))
        hrs = [scopy(3, j, hpart.at[pl.ds(snap_peer(sme, j, n_snap) * hw, hw)], hslots.at[j - 1]) for j in range(1, n_snap)]
        start(hrs)
        hag = [scopy(4, j, hred, hfull.at[pl.ds(sme * hw, hw)]) for j in range(1, n_snap)]

        def hess_share():
            finish(hrs)
            own = hpart[pl.ds(sme * hw, hw), :]
            for j in range(1, n_snap):
                own = own + hslots[j - 1]
            hred[...] = own
            hfull[pl.ds(sme * hw, hw), :] = own
            start(hag)
        limit = find_limit(2, error_pass(), hess_share, nothing)

        def moment(t, carry):
            j = n_snap - 1 - t
            q = snap_peer(sme, j, n_snap)
            part = pl.ds(pl.multiple_of(q * rw, rw), rw)
            hi, lo = split(jnp.clip(e[part, :], -limit, limit))
            mom[j] = quads(dot(jnp.concatenate([hi, lo], 0), ctcat[...]))

            @pl.when(j > 0)
            def _():
                scopy(5, j, mom.at[j], mom_slots.at[j - 1]).start()
            return carry
        lax.fori_loop(0, n_snap, moment, 0)
        finish(hag)
        hfull[...] = hfull[...] + eye
        sweep(hfull, 0, rank)
        finish([scopy(5, j, mom.at[j], mom_slots.at[j - 1]) for j in range(1, n_snap)])
        share = mom[0]
        for j in range(1, n_snap):
            share = share + mom_slots[j - 1]
        step = jnp.dot(share, hfull[...], preferred_element_type=F32, precision=lax.Precision.HIGHEST)
        m_out[own_rows, :] = m_out[own_rows, :] - step
        copies = [scopy(6, j, m_out.at[own_rows], m_out.at[own_rows]) for j in range(1, n_snap)]
        start(copies)
        finish(copies)

        @pl.when(o < OUTER - 1)
        def _():
            prepare_modes()
        return carry
    lax.fori_loop(0, OUTER, outer, 0)
    c_out[...] = c_out[...] * jnp.sqrt(jnp.float32(points))


def shards(n_pts, n_snap, snapshots, modes_init, coefs_init):
    rows, width = snapshots.shape
    rank = modes_init.shape[1]
    cw, rw, gw, hw = width // n_pts, rows // n_snap, rank // n_pts, rank // n_snap
    vmem = pltpu.VMEM
    scratch = [
        vmem((rows, width), F32), vmem((rows, width), F32),
        vmem((rows, 2 * rank), BF16), vmem((2 * rank, rows), BF16),
        vmem((2 * rank, width), BF16), vmem((width, 2 * rank), BF16),
        vmem((8, 256), F32),
        vmem((rank, rank), F32), vmem((n_pts - 1, gw, rank), F32), vmem((gw, rank), F32), vmem((rank, rank), F32),
        vmem((rank, rank), F32), vmem((n_snap - 1, hw, rank), F32), vmem((hw, rank), F32), vmem((rank, rank), F32),
        vmem((3, 8, 128), F32), vmem((3, n_pts - 1, 8, 128), F32),
        vmem((3, 8, 128), F32), vmem((3, n_snap - 1, 8, 128), F32),
        vmem((n_pts, rank, cw), F32), vmem((INNER, n_pts - 1, rank, cw), F32),
        vmem((n_snap, rw, rank), F32), vmem((n_snap - 1, rw, rank), F32),
        pltpu.SemaphoreType.DMA,
        pltpu.SemaphoreType.DMA((9, n_pts - 1)), pltpu.SemaphoreType.DMA((9, n_pts - 1)),
        pltpu.SemaphoreType.DMA((7, n_snap - 1)), pltpu.SemaphoreType.DMA((7, n_snap - 1)),
    ]
    return pl.pallas_call(
        functools.partial(kernel, n_pts, n_snap),
        out_shape=(jax.ShapeDtypeStruct((rows, rank), F32), jax.ShapeDtypeStruct((rank, width), F32)),
        in_specs=[pl.BlockSpec(memory_space=pl.ANY)] + [pl.BlockSpec(memory_space=vmem)] * 2,
        out_specs=(pl.BlockSpec(memory_space=vmem), pl.BlockSpec(memory_space=vmem)),
        scratch_shapes=scratch,
        compiler_params=pltpu.CompilerParams(collective_id=0, has_side_effects=True, vmem_limit_bytes=60 * 1024 * 1024),
    )(snapshots, modes_init, coefs_init)


def solution(mesh):
    in_specs = (P("pts", "snap"), P("pts", None), P(None, "snap"))
    out_specs = (P("pts", None), P(None, "snap"))
    body = functools.partial(shards, mesh.shape["pts"], mesh.shape["snap"])
    return jax.shard_map(body, mesh=mesh, in_specs=in_specs, out_specs=out_specs, check_vma=False)
```

```python
import functools

import jax
import jax.numpy as jnp
from jax import lax
from jax.experimental import pallas as pl
from jax.experimental.pallas import tpu as pltpu
from jax.sharding import PartitionSpec as P

OUTER = 2
INNER = 2
PIVOTS = 4
CHUNK = 128

HUBER = 1.345
RIDGE = 0.01

F32 = jnp.float32
BF16 = jnp.bfloat16
MESH = pl.DeviceIdType.MESH


def split(x):
    hi = x.astype(BF16)
    lo = (x - hi.astype(F32)).astype(BF16)
    return hi, lo


def dot(a, b):
    return jnp.dot(a, b, preferred_element_type=F32)


def quads(x):
    r, c = x.shape[0] // 2, x.shape[1] // 2
    return (x[:r, :c] + x[:r, c:]) + (x[r:, :c] + x[r:, c:])


def pts_peer(me, j, n):
    if n % 2:
        return lax.rem(me + j, n)
    x, c = me // 2, lax.rem(me, 2)
    return lax.rem(x + j // 2, n // 2) * 2 + lax.rem(c + lax.rem(j, 2), 2)


def snap_peer(me, j, n):
    return lax.rem(me + j, n)


def kernel(n_pts, n_snap, s_hbm, m_in, c_in, m_out, c_out,
           s, e, mcat, mtcat, ccat, ctcat, sq,
           gpart, gslots, gred, gfull, hpart, hslots, hred, hfull,
           tile_p, slots_p, tile_s, slots_s, cpart, cslots, xslots, ypart, yslots, zpart, zslots,
           load_sem, p_send, p_recv, s_send, s_recv, c_send, c_recv, x_send, x_recv,
           y_send, y_recv, z_send, z_recv):
    rows, width = s.shape
    rank = m_in.shape[1]
    pme = lax.axis_index("pts")
    sme = lax.axis_index("snap")
    rw = rows // n_snap
    half = width // 2
    chunks = half // CHUNK
    n_x, n_z = n_pts // 2, n_snap // 2
    px, core = pme // 2, lax.rem(pme, 2)
    sz, sy = sme // 2, lax.rem(sme, 2)
    gw = rank // n_pts
    hw = rank // n_snap
    count = float(rows * n_pts * width * n_snap)
    step_cols = 256

    load = pltpu.make_async_copy(s_hbm, s, load_sem)
    load.start()

    barrier = pltpu.get_barrier_semaphore()
    for j in range(1, n_pts):
        pl.semaphore_signal(barrier, inc=1, device_id={"pts": pts_peer(pme, j, n_pts)}, device_id_type=MESH)
    for j in range(1, n_snap):
        pl.semaphore_signal(barrier, inc=1, device_id={"snap": snap_peer(sme, j, n_snap)}, device_id_type=MESH)
    m_out[...] = m_in[...]
    c_out[...] = c_in[...]
    pl.semaphore_wait(barrier, n_pts - 1 + n_snap - 1)

    def pcopy(site, j, src, dst):
        return pltpu.make_async_remote_copy(
            src_ref=src, dst_ref=dst, send_sem=p_send.at[site, j - 1], recv_sem=p_recv.at[site, j - 1],
            device_id={"pts": pts_peer(pme, j, n_pts)}, device_id_type=MESH)

    def scopy(site, j, src, dst):
        return pltpu.make_async_remote_copy(
            src_ref=src, dst_ref=dst, send_sem=s_send.at[site, j - 1], recv_sem=s_recv.at[site, j - 1],
            device_id={"snap": snap_peer(sme, j, n_snap)}, device_id_type=MESH)

    def ccopy(site, k, src, dst):
        return pltpu.make_async_remote_copy(
            src_ref=src, dst_ref=dst, send_sem=c_send.at[site, k], recv_sem=c_recv.at[site, k],
            device_id={"pts": px * 2 + 1 - core}, device_id_type=MESH)

    def xcopy(site, k, d):
        ref = xslots.at[site, px, k]
        return pltpu.make_async_remote_copy(
            src_ref=ref, dst_ref=ref, send_sem=x_send.at[site, k, d - 1], recv_sem=x_recv.at[site, k, d - 1],
            device_id={"pts": lax.rem(px + d, n_x) * 2 + core}, device_id_type=MESH)

    def ycopy(site, d, src, dst):
        return pltpu.make_async_remote_copy(
            src_ref=src, dst_ref=dst, send_sem=y_send.at[site, d], recv_sem=y_recv.at[site, d],
            device_id={"snap": sz * 2 + 1 - sy}, device_id_type=MESH)

    def zcopy(site, d, src, dst):
        return pltpu.make_async_remote_copy(
            src_ref=src, dst_ref=dst, send_sem=z_send.at[site, d - 1], recv_sem=z_recv.at[site, d - 1],
            device_id={"snap": lax.rem(sz + d, n_z) * 2 + sy}, device_id_type=MESH)

    def col_chunk(which, k):
        return pl.ds(pl.multiple_of(which * half + k * CHUNK, CHUNK), CHUNK)

    def row_block(d, which):
        return pl.ds(pl.multiple_of((lax.rem(sz + d, n_z) * 2 + which) * rw, rw), rw)

    def start(copies):
        for copy in copies:
            copy.start()

    def finish(copies):
        for copy in copies:
            copy.wait_recv()
        for copy in copies:
            copy.wait_send()

    def prepare_modes():
        m = m_out[...]
        hi, lo = split(m)
        mcat[:, :rank] = hi
        mcat[:, rank:] = lo
        hi, lo = split(m.T)
        mtcat[:rank, :] = hi
        mtcat[rank:, :] = lo

    def prepare_coefs():
        hi, lo = split(c_out[...])
        ccat[:rank, :] = hi
        ccat[rank:, :] = lo

    def sweep(ref, lo, hi):
        lane = lax.broadcasted_iota(jnp.int32, (rank, rank), 1)
        sub = lax.broadcasted_iota(jnp.int32, (rank, rank), 0)
        lane_row = lax.broadcasted_iota(jnp.int32, (1, rank), 1)
        sub_col = lax.broadcasted_iota(jnp.int32, (rank, 1), 0)

        def body(t, carry):
            k = t * PIVOTS
            full = ref[...]
            cols = [jnp.sum(jnp.where(lane == k + p, full, 0.0), axis=1, keepdims=True) for p in range(PIVOTS)]
            rws = [ref[pl.ds(k + p, 1), :] for p in range(PIVOTS)]
            blk = {}
            for p in range(PIVOTS):
                for q in range(p, PIVOTS):
                    blk[p, q] = jnp.sum(jnp.where(lane_row == k + q, rws[p], 0.0), axis=1, keepdims=True)
            for p in range(PIVOTS):
                inv = 1.0 / blk[p, p]
                row, col = rws[p], cols[p]
                for q in range(p + 1, PIVOTS):
                    f = blk[p, q] * inv
                    rws[q] = jnp.where(lane_row == k + p, f, rws[q] - f * row)
                    cols[q] = jnp.where(sub_col == k + p, f, cols[q] - f * col)
                    for u in range(q, PIVOTS):
                        blk[q, u] = blk[q, u] - f * blk[p, u]
                rowd = row * inv
                full = jnp.where(lane == k + p, col * inv, full - col * rowd)
                full = jnp.where(sub == k + p, jnp.where(lane_row == k + p, -inv, rowd), full)
            ref[...] = full
            return carry
        lax.fori_loop(lo // PIVOTS, hi // PIVOTS, body, 0)

    def error_pass():
        sq[...] = jnp.zeros_like(sq)

        def body(t, carry):
            cols = pl.ds(pl.multiple_of(t * step_cols, step_cols), step_cols)
            c = ccat[:, cols]
            hi, lo = mcat[:, :rank], mcat[:, rank:]
            fit = dot(jnp.concatenate([hi, hi], 1), c) + dot(jnp.concatenate([lo, lo], 1), c)
            err = s[:, cols] - fit
            e[:, cols] = err
            sq[...] += jnp.sum((err * err).reshape(rows // 8, 8, step_cols), axis=0)
            return carry
        lax.fori_loop(0, width // step_cols, body, 0)
        acc = sq[:, :128]
        for k in range(1, step_cols // 128):
            acc = acc + sq[:, k * 128:(k + 1) * 128]
        return acc

    def find_limit(use, acc, fill_p, fill_s):
        tile_p[use] = acc
        copies = [pcopy(use, j, tile_p.at[use], slots_p.at[use, j - 1]) for j in range(1, n_pts)]
        start(copies)
        fill_p()
        finish(copies)
        acc = tile_p[use]
        for j in range(1, n_pts):
            acc = acc + slots_p[use, j - 1]
        tile_s[use] = acc
        copies = [scopy(use, j, tile_s.at[use], slots_s.at[use, j - 1]) for j in range(1, n_snap)]
        start(copies)
        fill_s()
        finish(copies)
        acc = tile_s[use]
        for j in range(1, n_snap):
            acc = acc + slots_s[use, j - 1]
        total = jnp.sum(jnp.sum(acc, axis=0, keepdims=True), axis=1, keepdims=True)
        return HUBER * jnp.sqrt(total / count + 1e-06)

    def nothing():
        return None

    eye = (lax.broadcasted_iota(jnp.int32, (rank, rank), 0)
           == lax.broadcasted_iota(jnp.int32, (rank, rank), 1)).astype(F32) * RIDGE

    prepare_modes()
    prepare_coefs()
    load.wait()

    def outer(o, carry):
        gpart[...] = quads(dot(mtcat[...], mcat[...]))
        grs = [pcopy(3, j, gpart.at[pl.ds(pts_peer(pme, j, n_pts) * gw, gw)], gslots.at[j - 1]) for j in range(1, n_pts)]
        start(grs)
        gag = [pcopy(4, j, gred, gfull.at[pl.ds(pme * gw, gw)]) for j in range(1, n_pts)]

        for inner in range(INNER):
            acc = error_pass()

            def gram_share():
                finish(grs)
                own = gpart[pl.ds(pme * gw, gw), :]
                for j in range(1, n_pts):
                    own = own + gslots[j - 1]
                gred[...] = own
                gfull[pl.ds(pme * gw, gw), :] = own
                start(gag)

            def gram_sweep():
                finish(gag)
                gfull[...] = gfull[...] + eye
                sweep(gfull, 0, rank // 2)
            first = inner == 0
            limit = find_limit(inner, acc, gram_share if first else nothing, gram_sweep if first else nothing)

            def product(cols):
                hi, lo = split(jnp.clip(e[:, cols], -limit, limit))
                return quads(dot(mtcat[...], jnp.concatenate([hi, lo], 1)))

            def give(k):
                return ccopy(inner, k, cpart.at[k], cslots.at[inner, k])

            def spread(k):
                ref = c_out.at[:, col_chunk(core, k)]
                return ccopy(INNER + inner, k, ref, ref)

            def theirs(k, carry):
                cpart[k] = product(col_chunk(1 - core, k))
                give(k).start()
                return carry
            lax.fori_loop(0, chunks, theirs, 0)

            def ours(k, carry):
                mine = product(col_chunk(core, k))
                give(k).wait_recv()
                xslots[inner, px, k] = mine + cslots[inner, k]
                for d in range(1, n_x):
                    xcopy(inner, k, d).start()
                return carry
            lax.fori_loop(0, chunks, ours, 0)
            if first:
                sweep(gfull, rank // 2, rank)

            def update(k, carry):
                for d in range(1, n_x):
                    xcopy(inner, k, d).wait_recv()
                share = xslots[inner, 0, k]
                for x in range(1, n_x):
                    share = share + xslots[inner, x, k]
                step = jnp.dot(gfull[...], share, preferred_element_type=F32, precision=lax.Precision.HIGHEST)
                cols = col_chunk(core, k)
                c_out[:, cols] = c_out[:, cols] - step
                spread(k).start()
                return carry
            lax.fori_loop(0, chunks, update, 0)

            def settle(k, carry):
                spread(k).wait_recv()
                spread(k).wait_send()
                give(k).wait_send()
                for d in range(1, n_x):
                    xcopy(inner, k, d).wait_send()
                return carry
            lax.fori_loop(0, chunks, settle, 0)
            prepare_coefs()

        hi, lo = split(c_out[...].T)
        ctcat[:, :rank] = hi
        ctcat[:, rank:] = lo
        hpart[...] = quads(dot(ccat[...], ctcat[...]))
        hrs = [scopy(3, j, hpart.at[pl.ds(snap_peer(sme, j, n_snap) * hw, hw)], hslots.at[j - 1]) for j in range(1, n_snap)]
        start(hrs)
        hag = [scopy(4, j, hred, hfull.at[pl.ds(sme * hw, hw)]) for j in range(1, n_snap)]

        def hess_share():
            finish(hrs)
            own = hpart[pl.ds(sme * hw, hw), :]
            for j in range(1, n_snap):
                own = own + hslots[j - 1]
            hred[...] = own
            hfull[pl.ds(sme * hw, hw), :] = own
            start(hag)
        limit = find_limit(2, error_pass(), hess_share, nothing)

        def moment(part):
            hi, lo = split(jnp.clip(e[part, :], -limit, limit))
            return quads(dot(jnp.concatenate([hi, lo], 0), ctcat[...]))

        def over_y(d):
            return ycopy(0, d, ypart.at[d], yslots.at[d])

        def over_z(d):
            return zcopy(0, d, zpart.at[d], zslots.at[d - 1])

        def theirs(t, carry):
            d = n_z - 1 - t
            ypart[d] = moment(row_block(d, 1 - sy))
            over_y(d).start()
            return carry
        lax.fori_loop(0, n_z, theirs, 0)

        def ours(t, carry):
            d = n_z - 1 - t
            mine = moment(row_block(d, sy))
            over_y(d).wait_recv()
            zpart[d] = mine + yslots[d]

            @pl.when(d > 0)
            def _():
                over_z(d).start()
            return carry
        lax.fori_loop(0, n_z, ours, 0)
        finish(hag)
        hfull[...] = hfull[...] + eye
        sweep(hfull, 0, rank)
        for d in range(1, n_z):
            over_z(d).wait_recv()
        share = zpart[0]
        for d in range(1, n_z):
            share = share + zslots[d - 1]
        step = jnp.dot(share, hfull[...], preferred_element_type=F32, precision=lax.Precision.HIGHEST)
        own_rows = row_block(0, sy)
        m_out[own_rows, :] = m_out[own_rows, :] - step
        own_ref = m_out.at[own_rows]
        order = sorted(range(1, n_z), key=lambda d: -min(d, n_z - d))
        for d in order:
            zcopy(1, d, own_ref, own_ref).start()
        ycopy(1, 0, own_ref, own_ref).start()

        def pass_on(d):
            ref = m_out.at[row_block(n_z - d, sy)]
            return ycopy(1, d, ref, ref)
        for d in sorted(range(1, n_z), key=lambda d: min(d, n_z - d)):
            zcopy(1, d, own_ref, own_ref).wait_recv()
            pass_on(d).start()
        ycopy(1, 0, own_ref, own_ref).wait_recv()
        for d in range(1, n_z):
            pass_on(d).wait_recv()
        ycopy(1, 0, own_ref, own_ref).wait_send()
        over_y(0).wait_send()
        for d in range(1, n_z):
            pass_on(d).wait_send()
            over_y(d).wait_send()
            over_z(d).wait_send()
            zcopy(1, d, own_ref, own_ref).wait_send()

        @pl.when(o < OUTER - 1)
        def _():
            prepare_modes()
        return carry
    lax.fori_loop(0, OUTER, outer, 0)


def shards(n_pts, n_snap, snapshots, modes_init, coefs_init):
    rows, width = snapshots.shape
    rank = modes_init.shape[1]
    rw, gw, hw = rows // n_snap, rank // n_pts, rank // n_snap
    chunks, n_x, n_z = width // 2 // CHUNK, n_pts // 2, n_snap // 2
    points = float(rows * n_pts)
    vmem = pltpu.VMEM
    scratch = [
        vmem((rows, width), F32), vmem((rows, width), F32),
        vmem((rows, 2 * rank), BF16), vmem((2 * rank, rows), BF16),
        vmem((2 * rank, width), BF16), vmem((width, 2 * rank), BF16),
        vmem((8, 256), F32),
        vmem((rank, rank), F32), vmem((n_pts - 1, gw, rank), F32), vmem((gw, rank), F32), vmem((rank, rank), F32),
        vmem((rank, rank), F32), vmem((n_snap - 1, hw, rank), F32), vmem((hw, rank), F32), vmem((rank, rank), F32),
        vmem((3, 8, 128), F32), vmem((3, n_pts - 1, 8, 128), F32),
        vmem((3, 8, 128), F32), vmem((3, n_snap - 1, 8, 128), F32),
        vmem((chunks, rank, CHUNK), F32), vmem((INNER, chunks, rank, CHUNK), F32),
        vmem((INNER, n_x, chunks, rank, CHUNK), F32),
        vmem((n_z, rw, rank), F32), vmem((n_z, rw, rank), F32),
        vmem((n_z, rw, rank), F32), vmem((n_z - 1, rw, rank), F32),
        pltpu.SemaphoreType.DMA,
        pltpu.SemaphoreType.DMA((5, n_pts - 1)), pltpu.SemaphoreType.DMA((5, n_pts - 1)),
        pltpu.SemaphoreType.DMA((5, n_snap - 1)), pltpu.SemaphoreType.DMA((5, n_snap - 1)),
        pltpu.SemaphoreType.DMA((2 * INNER, chunks)), pltpu.SemaphoreType.DMA((2 * INNER, chunks)),
        pltpu.SemaphoreType.DMA((INNER, chunks, n_x - 1)), pltpu.SemaphoreType.DMA((INNER, chunks, n_x - 1)),
        pltpu.SemaphoreType.DMA((2, n_z)), pltpu.SemaphoreType.DMA((2, n_z)),
        pltpu.SemaphoreType.DMA((2, n_z - 1)), pltpu.SemaphoreType.DMA((2, n_z - 1)),
    ]
    modes, coefs = pl.pallas_call(
        functools.partial(kernel, n_pts, n_snap),
        out_shape=(jax.ShapeDtypeStruct((rows, rank), F32), jax.ShapeDtypeStruct((rank, width), F32)),
        in_specs=[pl.BlockSpec(memory_space=pl.ANY)] + [pl.BlockSpec(memory_space=vmem)] * 2,
        out_specs=(pl.BlockSpec(memory_space=vmem), pl.BlockSpec(memory_space=vmem)),
        scratch_shapes=scratch,
        compiler_params=pltpu.CompilerParams(collective_id=0, has_side_effects=True, vmem_limit_bytes=60 * 1024 * 1024),
    )(snapshots, modes_init, coefs_init)
    return modes, coefs * jnp.sqrt(jnp.float32(points))


def solution(mesh):
    in_specs = (P("pts", "snap"), P("pts", None), P(None, "snap"))
    out_specs = (P("pts", None), P(None, "snap"))
    body = functools.partial(shards, mesh.shape["pts"], mesh.shape["snap"])
    return jax.shard_map(body, mesh=mesh, in_specs=in_specs, out_specs=out_specs, check_vma=False)
```

```python
import functools

import jax
import jax.numpy as jnp
from jax import lax
from jax.experimental import pallas as pl
from jax.experimental.pallas import tpu as pltpu
from jax.sharding import PartitionSpec as P

OUTER = 2
INNER = 2
PIVOTS = 4
CHUNK = 128

HUBER = 1.345
RIDGE = 0.01

F32 = jnp.float32
BF16 = jnp.bfloat16
MESH = pl.DeviceIdType.MESH


def split(x):
    hi = x.astype(BF16)
    lo = (x - hi.astype(F32)).astype(BF16)
    return hi, lo


def dot(a, b):
    return jnp.dot(a, b, preferred_element_type=F32)


def quads(x):
    r, c = x.shape[0] // 2, x.shape[1] // 2
    return (x[:r, :c] + x[:r, c:]) + (x[r:, :c] + x[r:, c:])


def pts_peer(me, j, n):
    if n % 2:
        return lax.rem(me + j, n)
    x, c = me // 2, lax.rem(me, 2)
    return lax.rem(x + j // 2, n // 2) * 2 + lax.rem(c + lax.rem(j, 2), 2)


def snap_peer(me, j, n):
    return lax.rem(me + j, n)


def kernel(n_pts, n_snap, s_hbm, m_in, c_in, m_out, c_out,
           s, e, mcat, mtcat, ccat, ctcat, sq,
           gpart, gslots, gred, gfull, hpart, hslots, hred, hfull,
           tile_p, slots_p, tile_s, slots_s, cpart, cslots, xslots, ypart, yslots, zpart, zslots,
           load_sem, p_send, p_recv, s_send, s_recv, c_send, c_recv, x_send, x_recv,
           y_send, y_recv, z_send, z_recv):
    rows, width = s.shape
    rank = m_in.shape[1]
    pme = lax.axis_index("pts")
    sme = lax.axis_index("snap")
    rw = rows // n_snap
    half = width // 2
    chunks = half // CHUNK
    n_x, n_z = n_pts // 2, n_snap // 2
    px, core = pme // 2, lax.rem(pme, 2)
    sz, sy = sme // 2, lax.rem(sme, 2)
    gw = rank // n_pts
    hw = rank // n_snap
    count = float(rows * n_pts * width * n_snap)
    step_cols = 256

    load = pltpu.make_async_copy(s_hbm, s, load_sem)
    load.start()

    barrier = pltpu.get_barrier_semaphore()
    for j in range(1, n_pts):
        pl.semaphore_signal(barrier, inc=1, device_id={"pts": pts_peer(pme, j, n_pts)}, device_id_type=MESH)
    for j in range(1, n_snap):
        pl.semaphore_signal(barrier, inc=1, device_id={"snap": snap_peer(sme, j, n_snap)}, device_id_type=MESH)
    m_out[...] = m_in[...]
    c_out[...] = c_in[...]
    pl.semaphore_wait(barrier, n_pts - 1 + n_snap - 1)

    def pcopy(site, j, src, dst):
        return pltpu.make_async_remote_copy(
            src_ref=src, dst_ref=dst, send_sem=p_send.at[site, j - 1], recv_sem=p_recv.at[site, j - 1],
            device_id={"pts": pts_peer(pme, j, n_pts)}, device_id_type=MESH)

    def scopy(site, j, src, dst):
        return pltpu.make_async_remote_copy(
            src_ref=src, dst_ref=dst, send_sem=s_send.at[site, j - 1], recv_sem=s_recv.at[site, j - 1],
            device_id={"snap": snap_peer(sme, j, n_snap)}, device_id_type=MESH)

    def ccopy(site, k, src, dst):
        return pltpu.make_async_remote_copy(
            src_ref=src, dst_ref=dst, send_sem=c_send.at[site, k], recv_sem=c_recv.at[site, k],
            device_id={"pts": px * 2 + 1 - core}, device_id_type=MESH)

    def xcopy(site, k, d):
        ref = xslots.at[site, px, k]
        return pltpu.make_async_remote_copy(
            src_ref=ref, dst_ref=ref, send_sem=x_send.at[site, k, d - 1], recv_sem=x_recv.at[site, k, d - 1],
            device_id={"pts": lax.rem(px + d, n_x) * 2 + core}, device_id_type=MESH)

    def ycopy(site, d, src, dst):
        return pltpu.make_async_remote_copy(
            src_ref=src, dst_ref=dst, send_sem=y_send.at[site, d], recv_sem=y_recv.at[site, d],
            device_id={"snap": sz * 2 + 1 - sy}, device_id_type=MESH)

    def zcopy(site, d, src, dst):
        return pltpu.make_async_remote_copy(
            src_ref=src, dst_ref=dst, send_sem=z_send.at[site, d - 1], recv_sem=z_recv.at[site, d - 1],
            device_id={"snap": lax.rem(sz + d, n_z) * 2 + sy}, device_id_type=MESH)

    def col_chunk(which, k):
        return pl.ds(pl.multiple_of(which * half + k * CHUNK, CHUNK), CHUNK)

    def row_block(d, which):
        return pl.ds(pl.multiple_of((lax.rem(sz + d, n_z) * 2 + which) * rw, rw), rw)

    def start(copies):
        for copy in copies:
            copy.start()

    def finish(copies):
        for copy in copies:
            copy.wait_recv()
        for copy in copies:
            copy.wait_send()

    def prepare_modes():
        m = m_out[...]
        hi, lo = split(m)
        mcat[:, :rank] = hi
        mcat[:, rank:] = lo
        hi, lo = split(m.T)
        mtcat[:rank, :] = hi
        mtcat[rank:, :] = lo

    def prepare_coefs():
        hi, lo = split(c_out[...])
        ccat[:rank, :] = hi
        ccat[rank:, :] = lo

    def sweep(ref, base, steps):
        lane = lax.broadcasted_iota(jnp.int32, (rank, rank), 1)
        sub = lax.broadcasted_iota(jnp.int32, (rank, rank), 0)
        lane_row = lax.broadcasted_iota(jnp.int32, (1, rank), 1)
        sub_col = lax.broadcasted_iota(jnp.int32, (rank, 1), 0)

        def body(t, carry):
            k = (base + t) * PIVOTS
            full = ref[...]
            cols = [jnp.sum(jnp.where(lane == k + p, full, 0.0), axis=1, keepdims=True) for p in range(PIVOTS)]
            rws = [ref[pl.ds(k + p, 1), :] for p in range(PIVOTS)]
            blk = {}
            for p in range(PIVOTS):
                for q in range(p, PIVOTS):
                    blk[p, q] = jnp.sum(jnp.where(lane_row == k + q, rws[p], 0.0), axis=1, keepdims=True)
            for p in range(PIVOTS):
                inv = 1.0 / blk[p, p]
                row, col = rws[p], cols[p]
                for q in range(p + 1, PIVOTS):
                    f = blk[p, q] * inv
                    rws[q] = jnp.where(lane_row == k + p, f, rws[q] - f * row)
                    cols[q] = jnp.where(sub_col == k + p, f, cols[q] - f * col)
                    for u in range(q, PIVOTS):
                        blk[q, u] = blk[q, u] - f * blk[p, u]
                rowd = row * inv
                full = jnp.where(lane == k + p, col * inv, full - col * rowd)
                full = jnp.where(sub == k + p, jnp.where(lane_row == k + p, -inv, rowd), full)
            ref[...] = full
            return carry
        lax.fori_loop(0, steps, body, 0)

    def error_pass():
        sq[...] = jnp.zeros_like(sq)

        def body(t, carry):
            cols = pl.ds(pl.multiple_of(t * step_cols, step_cols), step_cols)
            c = ccat[:, cols]
            hi, lo = mcat[:, :rank], mcat[:, rank:]
            fit = dot(jnp.concatenate([hi, hi], 1), c) + dot(jnp.concatenate([lo, lo], 1), c)
            err = s[:, cols] - fit
            e[:, cols] = err
            sq[...] += jnp.sum((err * err).reshape(rows // 8, 8, step_cols), axis=0)
            return carry
        lax.fori_loop(0, width // step_cols, body, 0)
        acc = sq[:, :128]
        for k in range(1, step_cols // 128):
            acc = acc + sq[:, k * 128:(k + 1) * 128]
        return acc

    def find_limit(use, acc, fill_p, fill_s):
        tile_p[use] = acc
        copies = [pcopy(use, j, tile_p.at[use], slots_p.at[use, j - 1]) for j in range(1, n_pts)]
        start(copies)
        fill_p()
        finish(copies)
        acc = tile_p[use]
        for j in range(1, n_pts):
            acc = acc + slots_p[use, j - 1]
        tile_s[use] = acc
        copies = [scopy(use, j, tile_s.at[use], slots_s.at[use, j - 1]) for j in range(1, n_snap)]
        start(copies)
        fill_s()
        finish(copies)
        acc = tile_s[use]
        for j in range(1, n_snap):
            acc = acc + slots_s[use, j - 1]
        total = jnp.sum(jnp.sum(acc, axis=0, keepdims=True), axis=1, keepdims=True)
        return HUBER * jnp.sqrt(total / count + 1e-06)

    def nothing():
        return None

    eye = (lax.broadcasted_iota(jnp.int32, (rank, rank), 0)
           == lax.broadcasted_iota(jnp.int32, (rank, rank), 1)).astype(F32) * RIDGE

    prepare_modes()
    prepare_coefs()
    load.wait()

    def outer(o, carry):
        gpart[...] = quads(dot(mtcat[...], mcat[...]))
        grs = [pcopy(3, j, gpart.at[pl.ds(pts_peer(pme, j, n_pts) * gw, gw)], gslots.at[j - 1]) for j in range(1, n_pts)]
        start(grs)
        gag = [pcopy(4, j, gred, gfull.at[pl.ds(pme * gw, gw)]) for j in range(1, n_pts)]

        for inner in range(INNER):
            acc = error_pass()

            def gram_share():
                finish(grs)
                own = gpart[pl.ds(pme * gw, gw), :]
                for j in range(1, n_pts):
                    own = own + gslots[j - 1]
                gred[...] = own
                gfull[pl.ds(pme * gw, gw), :] = own
                start(gag)

            def gram_sweep():
                finish(gag)
                gfull[...] = gfull[...] + eye
                sweep(gfull, 0, rank // PIVOTS // 2)
            first = inner == 0
            limit = find_limit(inner, acc, gram_share if first else nothing, gram_sweep if first else nothing)

            def product(cols):
                hi, lo = split(jnp.clip(e[:, cols], -limit, limit))
                return quads(dot(mtcat[...], jnp.concatenate([hi, lo], 1)))

            def give(k):
                return ccopy(inner, k, cpart.at[k], cslots.at[inner, k])

            def spread(k):
                ref = c_out.at[:, col_chunk(core, k)]
                return ccopy(INNER + inner, k, ref, ref)

            def theirs(k, carry):
                cpart[k] = product(col_chunk(1 - core, k))
                give(k).start()
                return carry
            lax.fori_loop(0, chunks, theirs, 0)

            def ours(k, carry):
                mine = product(col_chunk(core, k))
                give(k).wait_recv()
                xslots[inner, px, k] = mine + cslots[inner, k]
                for d in range(1, n_x):
                    xcopy(inner, k, d).start()
                return carry
            lax.fori_loop(0, chunks, ours, 0)
            if first:
                sweep(gfull, rank // PIVOTS // 2, rank // PIVOTS // 2)

            def update(k, carry):
                for d in range(1, n_x):
                    xcopy(inner, k, d).wait_recv()
                share = xslots[inner, 0, k]
                for x in range(1, n_x):
                    share = share + xslots[inner, x, k]
                step = jnp.dot(gfull[...], share, preferred_element_type=F32, precision=lax.Precision.HIGHEST)
                cols = col_chunk(core, k)
                c_out[:, cols] = c_out[:, cols] - step
                spread(k).start()
                return carry
            lax.fori_loop(0, chunks, update, 0)

            def settle(k, carry):
                spread(k).wait_recv()
                spread(k).wait_send()
                give(k).wait_send()
                for d in range(1, n_x):
                    xcopy(inner, k, d).wait_send()
                return carry
            lax.fori_loop(0, chunks, settle, 0)
            prepare_coefs()

        hi, lo = split(c_out[...].T)
        ctcat[:, :rank] = hi
        ctcat[:, rank:] = lo
        hpart[...] = quads(dot(ccat[...], ctcat[...]))
        hrs = [scopy(3, j, hpart.at[pl.ds(snap_peer(sme, j, n_snap) * hw, hw)], hslots.at[j - 1]) for j in range(1, n_snap)]
        start(hrs)
        hag = [scopy(4, j, hred, hfull.at[pl.ds(sme * hw, hw)]) for j in range(1, n_snap)]

        def hess_share():
            finish(hrs)
            own = hpart[pl.ds(sme * hw, hw), :]
            for j in range(1, n_snap):
                own = own + hslots[j - 1]
            hred[...] = own
            hfull[pl.ds(sme * hw, hw), :] = own
            start(hag)
        limit = find_limit(2, error_pass(), hess_share, nothing)

        def moment(part):
            hi, lo = split(jnp.clip(e[part, :], -limit, limit))
            return quads(dot(jnp.concatenate([hi, lo], 0), ctcat[...]))

        def over_y(d):
            return ycopy(0, d, ypart.at[d], yslots.at[d])

        def over_z(d):
            return zcopy(0, d, zpart.at[d], zslots.at[d - 1])

        def theirs(t, carry):
            d = n_z - 1 - t
            ypart[d] = moment(row_block(d, 1 - sy))
            over_y(d).start()
            return carry
        lax.fori_loop(0, n_z, theirs, 0)

        finish(hag)
        hfull[...] = hfull[...] + eye
        early = rank // PIVOTS // 2 // n_z

        def ours(t, carry):
            d = n_z - 1 - t
            mine = moment(row_block(d, sy))
            sweep(hfull, t * early, early)
            over_y(d).wait_recv()
            zpart[d] = mine + yslots[d]

            @pl.when(d > 0)
            def _():
                over_z(d).start()
            return carry
        lax.fori_loop(0, n_z, ours, 0)
        sweep(hfull, early * n_z, rank // PIVOTS - early * n_z)
        for d in range(1, n_z):
            over_z(d).wait_recv()
        share = zpart[0]
        for d in range(1, n_z):
            share = share + zslots[d - 1]
        step = jnp.dot(share, hfull[...], preferred_element_type=F32, precision=lax.Precision.HIGHEST)
        own_rows = row_block(0, sy)
        m_out[own_rows, :] = m_out[own_rows, :] - step
        own_ref = m_out.at[own_rows]
        order = sorted(range(1, n_z), key=lambda d: -min(d, n_z - d))
        for d in order:
            zcopy(1, d, own_ref, own_ref).start()
        ycopy(1, 0, own_ref, own_ref).start()

        def pass_on(d):
            ref = m_out.at[row_block(n_z - d, sy)]
            return ycopy(1, d, ref, ref)
        for d in sorted(range(1, n_z), key=lambda d: min(d, n_z - d)):
            zcopy(1, d, own_ref, own_ref).wait_recv()
            pass_on(d).start()
        ycopy(1, 0, own_ref, own_ref).wait_recv()
        for d in range(1, n_z):
            pass_on(d).wait_recv()
        ycopy(1, 0, own_ref, own_ref).wait_send()
        over_y(0).wait_send()
        for d in range(1, n_z):
            pass_on(d).wait_send()
            over_y(d).wait_send()
            over_z(d).wait_send()
            zcopy(1, d, own_ref, own_ref).wait_send()

        @pl.when(o < OUTER - 1)
        def _():
            prepare_modes()
        return carry
    lax.fori_loop(0, OUTER, outer, 0)


def shards(n_pts, n_snap, snapshots, modes_init, coefs_init):
    rows, width = snapshots.shape
    rank = modes_init.shape[1]
    rw, gw, hw = rows // n_snap, rank // n_pts, rank // n_snap
    chunks, n_x, n_z = width // 2 // CHUNK, n_pts // 2, n_snap // 2
    points = float(rows * n_pts)
    vmem = pltpu.VMEM
    scratch = [
        vmem((rows, width), F32), vmem((rows, width), F32),
        vmem((rows, 2 * rank), BF16), vmem((2 * rank, rows), BF16),
        vmem((2 * rank, width), BF16), vmem((width, 2 * rank), BF16),
        vmem((8, 256), F32),
        vmem((rank, rank), F32), vmem((n_pts - 1, gw, rank), F32), vmem((gw, rank), F32), vmem((rank, rank), F32),
        vmem((rank, rank), F32), vmem((n_snap - 1, hw, rank), F32), vmem((hw, rank), F32), vmem((rank, rank), F32),
        vmem((3, 8, 128), F32), vmem((3, n_pts - 1, 8, 128), F32),
        vmem((3, 8, 128), F32), vmem((3, n_snap - 1, 8, 128), F32),
        vmem((chunks, rank, CHUNK), F32), vmem((INNER, chunks, rank, CHUNK), F32),
        vmem((INNER, n_x, chunks, rank, CHUNK), F32),
        vmem((n_z, rw, rank), F32), vmem((n_z, rw, rank), F32),
        vmem((n_z, rw, rank), F32), vmem((n_z - 1, rw, rank), F32),
        pltpu.SemaphoreType.DMA,
        pltpu.SemaphoreType.DMA((5, n_pts - 1)), pltpu.SemaphoreType.DMA((5, n_pts - 1)),
        pltpu.SemaphoreType.DMA((5, n_snap - 1)), pltpu.SemaphoreType.DMA((5, n_snap - 1)),
        pltpu.SemaphoreType.DMA((2 * INNER, chunks)), pltpu.SemaphoreType.DMA((2 * INNER, chunks)),
        pltpu.SemaphoreType.DMA((INNER, chunks, n_x - 1)), pltpu.SemaphoreType.DMA((INNER, chunks, n_x - 1)),
        pltpu.SemaphoreType.DMA((2, n_z)), pltpu.SemaphoreType.DMA((2, n_z)),
        pltpu.SemaphoreType.DMA((2, n_z - 1)), pltpu.SemaphoreType.DMA((2, n_z - 1)),
    ]
    modes, coefs = pl.pallas_call(
        functools.partial(kernel, n_pts, n_snap),
        out_shape=(jax.ShapeDtypeStruct((rows, rank), F32), jax.ShapeDtypeStruct((rank, width), F32)),
        in_specs=[pl.BlockSpec(memory_space=pl.ANY)] + [pl.BlockSpec(memory_space=vmem)] * 2,
        out_specs=(pl.BlockSpec(memory_space=vmem), pl.BlockSpec(memory_space=vmem)),
        scratch_shapes=scratch,
        compiler_params=pltpu.CompilerParams(collective_id=0, has_side_effects=True, vmem_limit_bytes=60 * 1024 * 1024),
    )(snapshots, modes_init, coefs_init)
    return modes, coefs * jnp.sqrt(jnp.float32(points))


def solution(mesh):
    in_specs = (P("pts", "snap"), P("pts", None), P(None, "snap"))
    out_specs = (P("pts", None), P(None, "snap"))
    body = functools.partial(shards, mesh.shape["pts"], mesh.shape["snap"])
    return jax.shard_map(body, mesh=mesh, in_specs=in_specs, out_specs=out_specs, check_vma=False)
```
